512 devices in a mesh: dp: 32 (over y, x), seq: 16 (over z, core).
Axes of the slice: x: 4, y: 8, z: 8, core: 2. Of those that a mesh axis runs over, the one named last changes fastest.
Arguments:
- queries: bfloat16 [32, 2048, 2048], P('dp', 'seq'), may hold values from -6 to 6
- keys_in: bfloat16 [32, 2048, 2048], P('dp', 'seq'), may hold values from -6 to 6
- values_in: bfloat16 [32, 2048, 2048], P('dp', 'seq'), may hold values from -6 to 6
- grad_out: bfloat16 [32, 2048, 2048], P('dp', 'seq'), may hold values from -6 to 6
- feat_w: bfloat16 [2, 16, 128, 128], replicated, may hold values from -0.5 to 0.5
Outputs:
- grad_queries: bfloat16 [32, 2048, 2048], P('dp', 'seq')
- grad_keys: bfloat16 [32, 2048, 2048], P('dp', 'seq')
- grad_values: bfloat16 [32, 2048, 2048], P('dp', 'seq')
- grad_feat: float32 [4096, 128], P('dp')
The draws below stay inside these ranges and needn't reach their ends.
All inputs are finite; a program needn't handle non-finite values.
Results may differ from the reference program's by a relative error of at most 0.0064.
Values sent between devices are 32-bit elements; how exact they have to be, the bound alone decides.
A program may use at most 128 MiB of HBM per device.

```python
import math
import jax
import jax.numpy as jnp
from jax import lax

H = 16
DH = 128
TOK_DEV = 128
LENGTH = 2048
REPLICAS = 32
N_DP = 32
N_SEQ = 16


def raised(values, stream_key, source, target, shards_of, factor):
    def block_of(axis_at):
        return (jnp.arange(values.shape[axis_at]) // (values.shape[axis_at] // shards_of)).reshape((-1,) + (1,) * (values.ndim - 1 - axis_at))

    near = jax.random.permutation(stream_key, shards_of)[block_of(target)]
    other_side = (block_of(target) + shards_of // 2) % shards_of
    return jnp.where((block_of(source) == near) | (block_of(source) == other_side), factor * values, values)


def steps_of(own_key, extent, shards, smallest, largest):
    def one(axis_at, parts):
        draws = jax.random.uniform(jax.random.fold_in(jax.random.fold_in(own_key, 6), axis_at), (parts,), jnp.float32, smallest / len(shards), largest / len(shards))
        return jnp.repeat(jnp.exp(draws), extent[axis_at] // parts).reshape((-1,) + (1,) * (len(extent) - axis_at - 1))

    level = one(*shards[0])
    for cut in shards[1:]:
        level = level * one(*cut)
    return level


def centred(rng, shape, scale, limit, split=(), held_as=jnp.bfloat16):
    level = steps_of(rng, shape, split, -0.22, 0.18) if split else 1.0
    drawn = jax.random.normal(rng, shape, jnp.float32) * scale * level
    return jnp.minimum(jnp.maximum(drawn, -limit), limit).astype(held_as)


def noise_with(rng, extent, deviation, bound, shards, heavy, kind=jnp.bfloat16):
    drawn = deviation * jax.random.normal(rng, extent, jnp.float32)
    if shards:
        drawn = drawn * steps_of(rng, extent, shards, -0.22, 0.18)
    return jnp.clip(raised(drawn, jax.random.fold_in(rng, 3), *heavy), -bound, bound).astype(kind)


def setup_inputs(seed: int = 0) -> dict:
    keys = jax.random.split(jax.random.key(seed), 6)
    return {
        "queries": noise_with(keys[0], (REPLICAS, LENGTH, H * DH), 1.0, 6.0, ((0, 32), (1, 16)), (0, 2, 32, 2.75)),
        "keys_in": noise_with(keys[1], (REPLICAS, LENGTH, H * DH), 1.0, 6.0, ((0, 32), (1, 16)), (0, 2, 32, 2.75)),
        "values_in": centred(keys[2], (REPLICAS, LENGTH, H * DH), 1.0, 6.0, ((0, 32), (1, 16))),
        "grad_out": centred(keys[3], (REPLICAS, LENGTH, H * DH), 1.0, 6.0, ((0, 32), (1, 16))),
        "feat_w": centred(keys[4], (2, H, DH, DH), DH ** -0.5, 0.5),
    }


def one_replica(args, weights):
    queries, keys_in, values_in, grad_out = args
    scale = 1.0 / math.sqrt(DH * TOK_DEV * N_SEQ)
    shape = (N_SEQ, TOK_DEV, H, DH)
    qh = queries.reshape(shape)
    kh = keys_in.reshape(shape)
    vh = values_in.reshape(shape)
    gh = grad_out.reshape(shape)
    wq = weights[0].astype(jnp.float32)
    wk = weights[1].astype(jnp.float32)
    fq = jnp.einsum('ctha,hab->cthb', qh.astype(jnp.float32), wq).astype(jnp.bfloat16)
    fk = jnp.einsum('ctha,hab->cthb', kh.astype(jnp.float32), wk).astype(jnp.bfloat16)
    fq32 = fq.astype(jnp.float32)
    fk32 = fk.astype(jnp.float32)
    v32 = vh.astype(jnp.float32)
    g32 = gh.astype(jnp.float32)
    causal = jnp.tril(jnp.ones((TOK_DEV, TOK_DEV), dtype=bool))
    p_mat = jnp.where(causal, scale * jnp.einsum('ctha,csha->chts', fq32, fk32), 0.0).astype(jnp.bfloat16)
    q_mat = jnp.where(causal, scale * jnp.einsum('ctha,csha->chts', g32, v32), 0.0).astype(jnp.bfloat16)
    sterm = jnp.einsum('ctha,cthb->chab', fk32, v32)
    gterm = jnp.einsum('ctha,cthb->chab', fq32, g32)
    zero = jnp.zeros((1, H, DH, DH), jnp.float32)
    prefix = jnp.concatenate([zero, jnp.cumsum(sterm, axis=0)[:-1]], axis=0)
    suffix = jnp.concatenate([jnp.cumsum(gterm[::-1], axis=0)[:-1][::-1], zero], axis=0)
    s_b = prefix.astype(jnp.bfloat16).astype(jnp.float32)
    g_b = suffix.astype(jnp.bfloat16).astype(jnp.float32)
    p32 = p_mat.astype(jnp.float32)
    q32 = q_mat.astype(jnp.float32)
    dfq = (scale * jnp.einsum('cthb,chab->ctha', g32, s_b) + jnp.einsum('chts,csha->ctha', q32, fk32)).astype(jnp.bfloat16)
    dfk = (scale * jnp.einsum('cthb,chab->ctha', v32, g_b) + jnp.einsum('chts,ctha->csha', q32, fq32)).astype(jnp.bfloat16)
    dvv = (scale * jnp.einsum('ctha,chab->cthb', fk32, g_b) + jnp.einsum('chts,cthb->cshb', p32, g32)).astype(jnp.bfloat16)
    dq = jnp.einsum('cthb,hab->ctha', dfq.astype(jnp.float32), wq).astype(jnp.bfloat16)
    dk = jnp.einsum('cthb,hab->ctha', dfk.astype(jnp.float32), wk).astype(jnp.bfloat16)
    dwq = jnp.einsum('ctha,cthb->hab', qh.astype(jnp.float32), dfq.astype(jnp.float32))
    dwk = jnp.einsum('ctha,cthb->hab', kh.astype(jnp.float32), dfk.astype(jnp.float32))
    flat = (N_SEQ * TOK_DEV, H * DH)
    return (dq.reshape(flat), dk.reshape(flat), dvv.reshape(flat), jnp.stack([dwq, dwk]))

def reference(queries, keys_in, values_in, grad_out, feat_w):
    grad_q, grad_k, grad_v, grad_w = lax.map(lambda item: one_replica(item, feat_w), (queries, keys_in, values_in, grad_out))
    gscale = 1.0 / math.sqrt(TOK_DEV * N_SEQ * N_DP)
    grad_feat = (lax.optimization_barrier(jnp.sum(grad_w, axis=0)) * gscale).reshape(2 * H * DH, DH)
    return (grad_q, grad_k, grad_v, grad_feat)
```

```python
import functools
import math

import jax
import jax.numpy as jnp
from jax import lax
from jax.experimental import pallas as pl
from jax.experimental.pallas import tpu as pltpu
from jax.sharding import PartitionSpec as P

MESH = pl.DeviceIdType.MESH
F32 = jnp.float32
BF16 = jnp.bfloat16


def dot(a, b, ca, cb):
    return lax.dot_general(a, b, (((ca,), (cb,)), ((), ())), preferred_element_type=F32)


def remote(src, dst, send, recv, where):
    return pltpu.make_async_remote_copy(
        src_ref=src, dst_ref=dst, send_sem=send, recv_sem=recv, device_id=where, device_id_type=MESH
    )


def attention_kernel(
    scale,
    chips,
    q_ref,
    k_ref,
    v_ref,
    g_ref,
    w_ref,
    dq_ref,
    dk_ref,
    dv_ref,
    wg_ref,
    fq_ref,
    fk_ref,
    terms,
    mate,
    chain,
    onward,
    states,
    lent,
    mate_send,
    mate_recv,
    chain_send,
    chain_recv,
    lent_send,
    lent_recv,
):
    heads = w_ref.shape[1]
    size = w_ref.shape[2]
    rows = q_ref.shape[0]
    count = 2 * chips
    seq = lax.axis_index("seq")
    z = seq // 2
    core = seq % 2
    own = 1 - core
    partner = seq + 1 - 2 * core
    nxt = (seq + 4 * core - 2 + count) % count
    prv = (seq - 4 * core + 2 + count) % count
    hop = z * core + (chips - 1 - z) * (1 - core)
    first = hop == 0
    last = hop == chips - 1

    barrier = pltpu.get_barrier_semaphore()
    for other in (partner, nxt, prv):
        pl.semaphore_signal(barrier, inc=1, device_id={"seq": other}, device_id_type=MESH)

    def cols(h):
        return pl.ds(pl.multiple_of(h * size, size), size)

    def mate_copy(h):
        return remote(
            terms.at[core, h], mate.at[h], mate_send.at[h], mate_recv.at[h], {"seq": partner}
        )

    def chain_copy(h):
        return remote(
            onward.at[h], chain.at[h], chain_send.at[h], chain_recv.at[h], {"seq": nxt}
        )

    def lent_copy(h):
        return remote(chain.at[h], lent.at[h], lent_send.at[h], lent_recv.at[h], {"seq": partner})

    def features(h):
        c = cols(h)
        fq = dot(q_ref[:, c], w_ref[0, h], 1, 0).astype(BF16)
        fk = dot(k_ref[:, c], w_ref[1, h], 1, 0).astype(BF16)
        fq_ref[:, c] = fq
        fk_ref[:, c] = fk
        terms[0, h] = dot(fk, v_ref[:, c], 0, 0)
        terms[1, h] = dot(fq, g_ref[:, c], 0, 0)

    features(0)
    features(1)
    pl.semaphore_wait(barrier, 3)

    @pl.when(first)
    def _():
        chain[...] = jnp.zeros_like(chain)

    mate_copy(0).start()
    mate_copy(1).start()

    def start(i, carry):
        features(2 * i)
        features(2 * i + 1)
        mate_copy(2 * i).start()
        mate_copy(2 * i + 1).start()
        return carry

    lax.fori_loop(1, heads // 2, start, 0)

    causal = lax.broadcasted_iota(jnp.int32, (rows, rows), 0) >= lax.broadcasted_iota(
        jnp.int32, (rows, rows), 1
    )

    def masked(a, b):
        return jnp.where(causal, scale * dot(a, b, 1, 1), 0.0).astype(BF16)

    def query_side(h, state):
        c = cols(h)
        g = g_ref[:, c]
        qm = masked(g, v_ref[:, c])
        dfq = (scale * dot(g, state, 1, 1) + dot(qm, fk_ref[:, c], 1, 0)).astype(BF16)
        dq_ref[:, c] = dot(dfq, w_ref[0, h], 1, 1).astype(BF16)
        wg_ref[:, h] = dot(q_ref[:, c], dfq, 0, 0).reshape(rows // 8, 8, size)

    def key_side(h, state):
        c = cols(h)
        g = g_ref[:, c]
        v = v_ref[:, c]
        fq = fq_ref[:, c]
        fk = fk_ref[:, c]
        qm = masked(g, v)
        pm = masked(fq, fk)
        dfk = (scale * dot(v, state, 1, 1) + dot(qm, fq, 0, 0)).astype(BF16)
        dv_ref[:, c] = (scale * dot(fk, state, 1, 0) + dot(pm, g, 0, 0)).astype(BF16)
        dk_ref[:, c] = dot(dfk, w_ref[1, h], 1, 1).astype(BF16)
        wg_ref[:, heads + h] = dot(k_ref[:, c], dfk, 0, 0).reshape(rows // 8, 8, size)

    def own_pair(i):
        @pl.when(core == 1)
        def _():
            for h in (2 * i, 2 * i + 1):
                query_side(h, states[h])

        @pl.when(core == 0)
        def _():
            for h in (2 * i, 2 * i + 1):
                key_side(h, states[h])

    def lent_pair(i):
        lent_copy(2 * i).wait_recv()
        lent_copy(2 * i + 1).wait_recv()

        @pl.when(core == 0)
        def _():
            for h in (2 * i, 2 * i + 1):
                query_side(h, lent[h].astype(BF16))

        @pl.when(core == 1)
        def _():
            for h in (2 * i, 2 * i + 1):
                key_side(h, lent[h].astype(BF16))

    early = jnp.clip(4 * hop - 2 * chips + 2, 0, heads // 2)

    def ahead(i, carry):
        @pl.when(i < early)
        def _():
            lent_pair(i)

        return carry

    lax.fori_loop(0, heads // 2, ahead, 0)

    def link(h):
        mate_copy(h).wait_recv()

        @pl.when(jnp.logical_not(first))
        def _():
            chain_copy(h).wait_recv()

        mine = chain[h] + mate[h]

        @pl.when(jnp.logical_not(last))
        def _():
            onward[h] = mine + terms[own, h]
            chain_copy(h).start()

        lent_copy(h).start()
        states[h] = mine.astype(BF16)

    def links(i, carry):
        link(2 * i)
        link(2 * i + 1)

        @pl.when(last)
        def _():
            own_pair(i)

        return carry

    lax.fori_loop(0, heads // 2, links, 0)

    def behind(i, carry):
        @pl.when(jnp.logical_not(last))
        def _():
            own_pair(i)

        return carry

    lax.fori_loop(0, heads // 2, behind, 0)

    def rest(i, carry):
        @pl.when(i >= early)
        def _():
            lent_pair(i)

        return carry

    lax.fori_loop(0, heads // 2, rest, 0)

    def drain(h, carry):
        mate_copy(h).wait_send()
        lent_copy(h).wait_send()

        @pl.when(jnp.logical_not(last))
        def _():
            chain_copy(h).wait_send()

        return carry

    lax.fori_loop(0, heads, drain, 0)


def attention(queries, keys_in, values_in, grad_out, feat_w, scale, chips):
    rows, width = queries.shape
    heads, size = feat_w.shape[1:3]
    vmem = pl.BlockSpec(memory_space=pltpu.VMEM)
    rowed = jax.ShapeDtypeStruct((rows, width), BF16)
    state = pltpu.VMEM((heads, size, size), F32)
    sem = pltpu.SemaphoreType.DMA((heads,))
    return pl.pallas_call(
        functools.partial(attention_kernel, scale, chips),
        out_shape=[
            rowed,
            rowed,
            rowed,
            jax.ShapeDtypeStruct((size // 8, 2 * heads, 8, size), F32),
        ],
        in_specs=[vmem] * 5,
        out_specs=[vmem] * 4,
        scratch_shapes=[
            pltpu.VMEM((rows, width), BF16),
            pltpu.VMEM((rows, width), BF16),
            pltpu.VMEM((2, heads, size, size), F32),
            state,
            state,
            state,
            pltpu.VMEM((heads, size, size), BF16),
            state,
            sem,
            sem,
            sem,
            sem,
            sem,
            sem,
        ],
        compiler_params=pltpu.CompilerParams(collective_id=0, has_side_effects=True),
        name="attention",
    )(queries, keys_in, values_in, grad_out, feat_w)


def reduce_kernel(
    nz,
    ny,
    nx,
    w_ref,
    out_ref,
    mate,
    up,
    up_in,
    down,
    down_in,
    mine,
    y_in,
    part,
    x_in,
    whole,
    mate_send,
    mate_recv,
    up_send,
    up_recv,
    down_send,
    down_recv,
    y_send,
    y_recv,
    x_send,
    x_recv,
    z_send,
    z_recv,
    last_send,
    last_recv,
):
    seq = lax.axis_index("seq")
    dp = lax.axis_index("dp")
    z = seq // 2
    core = seq % 2
    y = dp // nx
    x = dp % nx
    partner = {"seq": seq + 1 - 2 * core}

    def at_z(j):
        return {"seq": ((z + j + nz) % nz) * 2 + core}

    def at_y(j):
        return {"dp": ((y + j) % ny) * nx + x}

    def at_x(j):
        return {"dp": y * nx + (x + j) % nx}

    barrier = pltpu.get_barrier_semaphore()
    peers = [partner]
    peers += [at_z(j) for j in range(1, nz)]
    peers += [at_y(j) for j in range(1, ny)]
    peers += [at_x(j) for j in range(1, nx)]
    for peer in peers:
        pl.semaphore_signal(barrier, inc=1, device_id=peer, device_id_type=MESH)
    pl.semaphore_wait(barrier, len(peers))

    ups = nz // 2
    downs = nz - 1 - ups
    blocks = w_ref.shape[1]
    half = blocks // 2

    order = []
    for j in range(ups):
        order.append(ups - j)
        if j < downs:
            order.append(nz - (downs - j))
    order.append(0)
    mates = {}
    for j in order:
        t = (z + j) % nz
        mates[j] = remote(
            w_ref.at[(1 - core) * nz + t], mate.at[j], mate_send.at[j], mate_recv.at[j], partner
        )
        mates[j].start()

    waited = set()

    def local(j, span):
        if j not in waited:
            waited.add(j)
            mates[j].wait_recv()
        return w_ref[core * nz + (z + j) % nz, span] + mate[j, span]

    sends = []
    up_copies = {}
    down_copies = {}
    for step in range(ups):
        for part_no in range(2):
            span = pl.ds(part_no * half, half)
            for name, steps, buf, inbox, ss, rs, copies in (
                ("up", ups, up, up_in, up_send, up_recv, up_copies),
                ("down", downs, down, down_in, down_send, down_recv, down_copies),
            ):
                if step >= steps:
                    continue
                j = ups - step if name == "up" else nz - (downs - step)
                value = local(j, span)
                if step:
                    copies[step - 1, part_no].wait_recv()
                    value = value + inbox[step - 1, span]
                buf[step, span] = value
                copy = remote(
                    buf.at[step, span],
                    inbox.at[step, span],
                    ss.at[step, part_no],
                    rs.at[step, part_no],
                    at_z(1 if name == "up" else -1),
                )
                copy.start()
                copies[step, part_no] = copy
                sends.append(copy)

    y_copies = []
    for part_no in range(2):
        span = pl.ds(part_no * half, half)
        value = local(0, span)
        up_copies[ups - 1, part_no].wait_recv()
        down_copies[downs - 1, part_no].wait_recv()
        mine[span] = value + up_in[ups - 1, span] + down_in[downs - 1, span]

    for j in range(1, ny):
        there = (y + j) % ny
        copy = remote(
            mine.at[pl.ds(there * nx, nx)], y_in.at[j], y_send.at[j], y_recv.at[j], at_y(j)
        )
        copy.start()
        y_copies.append(copy)
    total = mine[pl.ds(y * nx, nx)]
    for j in range(1, ny):
        y_copies[j - 1].wait_recv()
        total = total + y_in[j]
    part[...] = total
    x_copies = []
    for j in range(1, nx):
        copy = remote(part.at[(x + j) % nx], x_in.at[j], x_send.at[j], x_recv.at[j], at_x(j))
        copy.start()
        x_copies.append(copy)
    total = part[x]
    for j in range(1, nx):
        x_copies[j - 1].wait_recv()
        total = total + x_in[j]
    whole[core, z] = total

    z_copies = []
    for j in range(1, nz):
        copy = remote(
            whole.at[core, z], whole.at[core, z], z_send.at[j], z_recv.at[j], at_z(j)
        )
        copy.start()
        z_copies.append(copy)
    for j in range(1, nz):
        z_copies[j - 1].wait_recv()
    copy = remote(whole.at[core], whole.at[core], last_send, last_recv, partner)
    copy.start()
    copy.wait_recv()
    out_ref[...] = whole[...]

    sends += y_copies + x_copies + z_copies + [copy] + [mates[j] for j in order]
    for copy in sends:
        copy.wait_send()


def reduce_grad(pieces, nz, ny, nx):
    groups, blocks, sub, size = pieces.shape
    vmem = pl.BlockSpec(memory_space=pltpu.VMEM)
    dma = pltpu.SemaphoreType.DMA
    ups = nz // 2
    downs = nz - 1 - ups
    return pl.pallas_call(
        functools.partial(reduce_kernel, nz, ny, nx),
        out_shape=jax.ShapeDtypeStruct((2, nz, sub, size), F32),
        in_specs=[vmem],
        out_specs=vmem,
        scratch_shapes=[
            pltpu.VMEM((nz, blocks, sub, size), F32),
            pltpu.VMEM((ups, blocks, sub, size), F32),
            pltpu.VMEM((ups, blocks, sub, size), F32),
            pltpu.VMEM((downs, blocks, sub, size), F32),
            pltpu.VMEM((downs, blocks, sub, size), F32),
            pltpu.VMEM((blocks, sub, size), F32),
            pltpu.VMEM((ny, nx, sub, size), F32),
            pltpu.VMEM((nx, sub, size), F32),
            pltpu.VMEM((nx, sub, size), F32),
            pltpu.VMEM((2, nz, sub, size), F32),
            dma((nz,)),
            dma((nz,)),
            dma((ups, 2)),
            dma((ups, 2)),
            dma((downs, 2)),
            dma((downs, 2)),
            dma((ny,)),
            dma((ny,)),
            dma((nx,)),
            dma((nx,)),
            dma((nz,)),
            dma((nz,)),
            dma,
            dma,
        ],
        compiler_params=pltpu.CompilerParams(collective_id=1, has_side_effects=True),
        name="reduce_grad",
    )(pieces)


def body(queries, keys_in, values_in, grad_out, feat_w):
    seq_count = lax.axis_size("seq")
    rep_count = lax.axis_size("dp")
    rows = queries.shape[1]
    hsize = feat_w.shape[2]
    scale = 1.0 / math.sqrt(hsize * rows * seq_count)
    gscale = 1.0 / math.sqrt(rows * seq_count * rep_count)
    nz = seq_count // 2
    nx = 4
    ny = rep_count // nx
    d_queries, d_keys, d_values, pieces = attention(
        queries[0], keys_in[0], values_in[0], grad_out[0], feat_w, scale, nz
    )
    owned = reduce_grad(pieces, nz, ny, nx).reshape(hsize, hsize)
    return (d_queries[None], d_keys[None], d_values[None], owned * gscale)


def solution(mesh):
    return jax.shard_map(
        body,
        mesh=mesh,
        in_specs=(
            P("dp", "seq", None),
            P("dp", "seq", None),
            P("dp", "seq", None),
            P("dp", "seq", None),
            P(),
        ),
        out_specs=(P("dp", "seq", None), P("dp", "seq", None), P("dp", "seq", None), P("dp", None)),
        check_vma=False,
    )
```

```python
import functools
import math

import jax
import jax.numpy as jnp
from jax import lax
from jax.experimental import pallas as pl
from jax.experimental.pallas import tpu as pltpu
from jax.sharding import PartitionSpec as P

MESH = pl.DeviceIdType.MESH
F32 = jnp.float32
BF16 = jnp.bfloat16


def dot(a, b, ca, cb):
    return lax.dot_general(a, b, (((ca,), (cb,)), ((), ())), preferred_element_type=F32)


def remote(src, dst, send, recv, where):
    return pltpu.make_async_remote_copy(
        src_ref=src, dst_ref=dst, send_sem=send, recv_sem=recv, device_id=where, device_id_type=MESH
    )


def attention_kernel(
    scale,
    chips,
    ny,
    nx,
    q_ref,
    k_ref,
    v_ref,
    g_ref,
    w_ref,
    dq_ref,
    dk_ref,
    dv_ref,
    out_ref,
    fq_ref,
    fk_ref,
    terms,
    mate,
    chain,
    onward,
    states,
    lent,
    mate_send,
    mate_recv,
    chain_send,
    chain_recv,
    lent_send,
    lent_recv,
    wg_ref,
    pair,
    up,
    up_in,
    down,
    down_in,
    mine_ref,
    y_in,
    part,
    x_in,
    whole,
    pair_send,
    pair_recv,
    up_send,
    up_recv,
    down_send,
    down_recv,
    y_send,
    y_recv,
    x_send,
    x_recv,
    z_send,
    z_recv,
    last_send,
    last_recv,
):
    heads = w_ref.shape[1]
    size = w_ref.shape[2]
    rows = q_ref.shape[0]
    count = 2 * chips
    seq = lax.axis_index("seq")
    z = seq // 2
    core = seq % 2
    own = 1 - core
    partner = seq + 1 - 2 * core
    nxt = (seq + 4 * core - 2 + count) % count
    hop = z * core + (chips - 1 - z) * (1 - core)
    first = hop == 0
    last = hop == chips - 1

    dp = lax.axis_index("dp")
    y = dp // nx
    x = dp % nx

    def at_z(j):
        return {"seq": ((z + j + chips) % chips) * 2 + core}

    def at_y(j):
        return {"dp": ((y + j) % ny) * nx + x}

    def at_x(j):
        return {"dp": y * nx + (x + j) % nx}

    barrier = pltpu.get_barrier_semaphore()
    peers = [{"seq": partner}]
    peers += [at_z(j) for j in range(1, chips)]
    peers += [at_y(j) for j in range(1, ny)]
    peers += [at_x(j) for j in range(1, nx)]
    for peer in peers:
        pl.semaphore_signal(barrier, inc=1, device_id=peer, device_id_type=MESH)

    def cols(h):
        return pl.ds(pl.multiple_of(h * size, size), size)

    def mate_copy(h):
        return remote(
            terms.at[core, h], mate.at[h], mate_send.at[h], mate_recv.at[h], {"seq": partner}
        )

    def chain_copy(h):
        return remote(
            onward.at[h], chain.at[h], chain_send.at[h], chain_recv.at[h], {"seq": nxt}
        )

    def lent_copy(h):
        return remote(chain.at[h], lent.at[h], lent_send.at[h], lent_recv.at[h], {"seq": partner})

    def features(h):
        c = cols(h)
        fq = dot(q_ref[:, c], w_ref[0, h], 1, 0).astype(BF16)
        fk = dot(k_ref[:, c], w_ref[1, h], 1, 0).astype(BF16)
        fq_ref[:, c] = fq
        fk_ref[:, c] = fk
        terms[0, h] = dot(fk, v_ref[:, c], 0, 0)
        terms[1, h] = dot(fq, g_ref[:, c], 0, 0)

    features(0)
    features(1)
    pl.semaphore_wait(barrier, len(peers))

    @pl.when(first)
    def _():
        chain[...] = jnp.zeros_like(chain)

    mate_copy(0).start()
    mate_copy(1).start()

    def start(i, carry):
        features(2 * i)
        features(2 * i + 1)
        mate_copy(2 * i).start()
        mate_copy(2 * i + 1).start()
        return carry

    lax.fori_loop(1, heads // 2, start, 0)

    causal = lax.broadcasted_iota(jnp.int32, (rows, rows), 0) >= lax.broadcasted_iota(
        jnp.int32, (rows, rows), 1
    )

    def masked(a, b):
        return jnp.where(causal, scale * dot(a, b, 1, 1), 0.0).astype(BF16)

    def block(h, side):
        return (h // nx) * (2 * nx) + side * nx + h % nx

    def pair_copy(d):
        return remote(
            wg_ref.at[pl.ds((1 - core) * chips, chips), d],
            pair.at[:, d],
            pair_send.at[d],
            pair_recv.at[d],
            {"seq": partner},
        )

    def query_side(h, state):
        c = cols(h)
        g = g_ref[:, c]
        qm = masked(g, v_ref[:, c])
        dfq = (scale * dot(g, state, 1, 1) + dot(qm, fk_ref[:, c], 1, 0)).astype(BF16)
        dq_ref[:, c] = dot(dfq, w_ref[0, h], 1, 1).astype(BF16)
        wg_ref[:, block(h, 0)] = dot(q_ref[:, c], dfq, 0, 0).reshape(rows // 8, 8, size)

    def key_side(h, state):
        c = cols(h)
        g = g_ref[:, c]
        v = v_ref[:, c]
        fq = fq_ref[:, c]
        fk = fk_ref[:, c]
        qm = masked(g, v)
        pm = masked(fq, fk)
        dfk = (scale * dot(v, state, 1, 1) + dot(qm, fq, 0, 0)).astype(BF16)
        dv_ref[:, c] = (scale * dot(fk, state, 1, 0) + dot(pm, g, 0, 0)).astype(BF16)
        dk_ref[:, c] = dot(dfk, w_ref[1, h], 1, 1).astype(BF16)
        wg_ref[:, block(h, 1)] = dot(k_ref[:, c], dfk, 0, 0).reshape(rows // 8, 8, size)

    def own_pair(i):
        @pl.when(core == 1)
        def _():
            for h in (2 * i, 2 * i + 1):
                query_side(h, states[h])

        @pl.when(core == 0)
        def _():
            for h in (2 * i, 2 * i + 1):
                key_side(h, states[h])

        for h in (2 * i, 2 * i + 1):
            pair_copy(block(h, 1 - core)).start()

    def lent_pair(i):
        lent_copy(2 * i).wait_recv()
        lent_copy(2 * i + 1).wait_recv()

        @pl.when(core == 0)
        def _():
            for h in (2 * i, 2 * i + 1):
                query_side(h, lent[h].astype(BF16))

        @pl.when(core == 1)
        def _():
            for h in (2 * i, 2 * i + 1):
                key_side(h, lent[h].astype(BF16))

        for h in (2 * i, 2 * i + 1):
            pair_copy(block(h, core)).start()

    early = jnp.clip(4 * hop - 2 * chips + 2, 0, heads // 2)

    def ahead(i, carry):
        @pl.when(i < early)
        def _():
            lent_pair(i)

        return carry

    lax.fori_loop(0, heads // 2, ahead, 0)

    def link(h):
        mate_copy(h).wait_recv()

        @pl.when(jnp.logical_not(first))
        def _():
            chain_copy(h).wait_recv()

        mine = chain[h] + mate[h]

        @pl.when(jnp.logical_not(last))
        def _():
            onward[h] = mine + terms[own, h]
            chain_copy(h).start()

        lent_copy(h).start()
        states[h] = mine.astype(BF16)

    def links(i, carry):
        link(2 * i)
        link(2 * i + 1)

        @pl.when(last)
        def _():
            own_pair(i)

        return carry

    lax.fori_loop(0, heads // 2, links, 0)

    def gradients(i):
        @pl.when(jnp.logical_not(last))
        def _():
            own_pair(i)

        @pl.when(i >= early)
        def _():
            lent_pair(i)

    groups = heads // nx
    group = 2 * nx
    pairs = heads // 2 // groups
    ups = chips // 2
    downs = chips - 1 - ups

    def span_of(n):
        return pl.ds(pl.multiple_of(n * group, group), group)

    def local(j, span):
        t = (z + j) % chips
        return wg_ref[core * chips + t, span] + pair[t, span]

    def up_copy(step, n):
        span = span_of(n)
        return remote(
            up.at[step, span], up_in.at[step, span], up_send.at[step, n], up_recv.at[step, n], at_z(1)
        )

    def down_copy(step, n):
        span = span_of(n)
        return remote(
            down.at[step, span],
            down_in.at[step, span],
            down_send.at[step, n],
            down_recv.at[step, n],
            at_z(-1),
        )

    def advance(step, n):
        span = span_of(n)
        if step == 0:

            def arrived(d, carry):
                pair_copy(n * group + d).wait_recv()
                return carry

            lax.fori_loop(0, group, arrived, 0)
        if step < ups:
            value = local(ups - step, span)
            if step:
                up_copy(step - 1, n).wait_recv()
                value = value + up_in[step - 1, span]
            up[step, span] = value
            up_copy(step, n).start()
        if step < downs:
            value = local(chips - (downs - step), span)
            if step:
                down_copy(step - 1, n).wait_recv()
                value = value + down_in[step - 1, span]
            down[step, span] = value
            down_copy(step, n).start()
        if step == ups:
            up_copy(ups - 1, n).wait_recv()
            down_copy(downs - 1, n).wait_recv()
            mine_ref[span] = local(0, span) + up_in[ups - 1, span] + down_in[downs - 1, span]
            for side in range(2):
                there = side * groups + n

                @pl.when(there != y)
                def _():
                    y_copy((there - y + ny) % ny).start()

    def y_span(there):
        return pl.ds((there % groups) * group + (there // groups) * nx, nx)

    def y_copy(j):
        return remote(
            mine_ref.at[y_span((y + j) % ny)], y_in.at[j], y_send.at[j], y_recv.at[j], at_y(j)
        )

    def slot(s, carry):
        @pl.when(s < groups)
        def _():
            for p in range(pairs):
                gradients(pairs * s + p)

        for step in range(ups + 1):

            @pl.when((s >= step) & (s < step + groups))
            def _():
                advance(step, s - step)

        return carry

    lax.fori_loop(0, groups + ups, slot, 0)

    total = mine_ref[y_span(y)]
    for j in range(1, ny):
        y_copy(j).wait_recv()
        total = total + y_in[j]
    part[...] = total
    x_copies = []
    for j in range(1, nx):
        copy = remote(part.at[(x + j) % nx], x_in.at[j], x_send.at[j], x_recv.at[j], at_x(j))
        copy.start()
        x_copies.append(copy)
    total = part[x]
    for j in range(1, nx):
        x_copies[j - 1].wait_recv()
        total = total + x_in[j]
    whole[core, z] = total

    z_copies = []
    for j in range(1, chips):
        copy = remote(whole.at[core, z], whole.at[core, z], z_send.at[j], z_recv.at[j], at_z(j))
        copy.start()
        z_copies.append(copy)
    for copy in z_copies:
        copy.wait_recv()
    final = remote(whole.at[core], whole.at[core], last_send, last_recv, {"seq": partner})
    final.start()

    def drain(h, carry):
        mate_copy(h).wait_send()
        lent_copy(h).wait_send()

        @pl.when(jnp.logical_not(last))
        def _():
            chain_copy(h).wait_send()

        return carry

    lax.fori_loop(0, heads, drain, 0)

    def drain_blocks(d, carry):
        pair_copy(d).wait_send()
        return carry

    lax.fori_loop(0, 2 * heads, drain_blocks, 0)

    def drain_groups(n, carry):
        for step in range(ups):
            up_copy(step, n).wait_send()
        for step in range(downs):
            down_copy(step, n).wait_send()
        return carry

    lax.fori_loop(0, groups, drain_groups, 0)
    for j in range(1, ny):
        y_copy(j).wait_send()
    for copy in x_copies + z_copies:
        copy.wait_send()
    final.wait()
    out_ref[...] = whole[...]


def attention(queries, keys_in, values_in, grad_out, feat_w, scale, chips, ny, nx):
    rows, width = queries.shape
    heads, size = feat_w.shape[1:3]
    vmem = pl.BlockSpec(memory_space=pltpu.VMEM)
    rowed = jax.ShapeDtypeStruct((rows, width), BF16)
    state = pltpu.VMEM((heads, size, size), F32)
    dma = pltpu.SemaphoreType.DMA
    ups = chips // 2
    downs = chips - 1 - ups
    blocks = 2 * heads
    sub = size // (2 * chips)

    def pieces(*lead):
        return pltpu.VMEM((*lead, sub, size), F32)

    return pl.pallas_call(
        functools.partial(attention_kernel, scale, chips, ny, nx),
        out_shape=[rowed] * 3 + [jax.ShapeDtypeStruct((2, chips, sub, size), F32)],
        in_specs=[vmem] * 5,
        out_specs=[vmem] * 4,
        scratch_shapes=[
            pltpu.VMEM((rows, width), BF16),
            pltpu.VMEM((rows, width), BF16),
            pltpu.VMEM((2, heads, size, size), F32),
            state,
            state,
            state,
            pltpu.VMEM((heads, size, size), BF16),
            state,
        ]
        + [dma((heads,))] * 6
        + [
            pieces(2 * chips, blocks),
            pieces(chips, blocks),
            pieces(ups, blocks),
            pieces(ups, blocks),
            pieces(downs, blocks),
            pieces(downs, blocks),
            pieces(blocks),
            pieces(ny, nx),
            pieces(nx),
            pieces(nx),
            pieces(2, chips),
        ]
        + [dma((blocks,))] * 2
        + [dma((ups, heads // nx))] * 2
        + [dma((downs, heads // nx))] * 2
        + [dma((ny,))] * 2
        + [dma((nx,))] * 2
        + [dma((chips,))] * 2
        + [dma] * 2,
        compiler_params=pltpu.CompilerParams(collective_id=0, has_side_effects=True),
        name="attention",
    )(queries, keys_in, values_in, grad_out, feat_w)


def finish_kernel(gscale, a_ref, b_ref, c_ref, d_ref, oa_ref, ob_ref, oc_ref, od_ref):
    oa_ref[...] = a_ref[...]
    ob_ref[...] = b_ref[...]
    oc_ref[...] = c_ref[...]
    od_ref[...] = d_ref[...] * gscale


def finish(arrays, gscale, steps=2):
    specs = [
        pl.BlockSpec((a.shape[0] // steps, a.shape[1]), lambda i: (i, 0)) for a in arrays
    ]
    return pl.pallas_call(
        functools.partial(finish_kernel, gscale),
        grid=(steps,),
        out_shape=[jax.ShapeDtypeStruct(a.shape, a.dtype) for a in arrays],
        in_specs=specs,
        out_specs=specs,
        name="finish",
    )(*arrays)


def body(queries, keys_in, values_in, grad_out, feat_w):
    seq_count = lax.axis_size("seq")
    rep_count = lax.axis_size("dp")
    rows = queries.shape[1]
    hsize = feat_w.shape[2]
    scale = 1.0 / math.sqrt(hsize * rows * seq_count)
    gscale = 1.0 / math.sqrt(rows * seq_count * rep_count)
    nz = seq_count // 2
    nx = 4
    ny = rep_count // nx
    d_queries, d_keys, d_values, owned = attention(
        queries[0], keys_in[0], values_in[0], grad_out[0], feat_w, scale, nz, ny, nx
    )
    results = finish((d_queries, d_keys, d_values, owned.reshape(hsize, hsize)), gscale)
    return (results[0][None], results[1][None], results[2][None], results[3])


def solution(mesh):
    return jax.shard_map(
        body,
        mesh=mesh,
        in_specs=(
            P("dp", "seq", None),
            P("dp", "seq", None),
            P("dp", "seq", None),
            P("dp", "seq", None),
            P(),
        ),
        out_specs=(P("dp", "seq", None), P("dp", "seq", None), P("dp", "seq", None), P("dp", None)),
        check_vma=False,
    )
```

```python
import functools
import math

import jax
import jax.numpy as jnp
from jax import lax
from jax.experimental import pallas as pl
from jax.experimental.pallas import tpu as pltpu
from jax.sharding import PartitionSpec as P

SPLIT = 4
MESH = pl.DeviceIdType.MESH
F32 = jnp.float32
BF16 = jnp.bfloat16


def dot(a, b, ca, cb):
    return lax.dot_general(a, b, (((ca,), (cb,)), ((), ())), preferred_element_type=F32)


def remote(src, dst, send, recv, where):
    return pltpu.make_async_remote_copy(
        src_ref=src, dst_ref=dst, send_sem=send, recv_sem=recv, device_id=where, device_id_type=MESH
    )


def attention_kernel(
    scale,
    chips,
    ny,
    nx,
    q_ref,
    k_ref,
    v_ref,
    g_ref,
    w_ref,
    dq_ref,
    dk_ref,
    dv_ref,
    out_ref,
    fq_ref,
    fk_ref,
    terms,
    mate,
    chain,
    onward,
    states,
    lend,
    lent,
    mate_send,
    mate_recv,
    chain_send,
    chain_recv,
    lent_send,
    lent_recv,
    wg_ref,
    pair,
    up,
    up_in,
    down,
    down_in,
    mine_ref,
    y_in,
    part,
    x_in,
    whole,
    pair_send,
    pair_recv,
    up_send,
    up_recv,
    down_send,
    down_recv,
    y_send,
    y_recv,
    x_send,
    x_recv,
    z_send,
    z_recv,
):
    heads = w_ref.shape[1]
    size = w_ref.shape[2]
    rows = q_ref.shape[0]
    count = 2 * chips
    seq = lax.axis_index("seq")
    z = seq // 2
    core = seq % 2
    role = 1 - core
    own = 1 - role
    partner = seq + 1 - 2 * core
    nxt = (seq + 4 * role - 2 + count) % count
    hop = z * role + (chips - 1 - z) * (1 - role)
    first = hop == 0
    last = hop == chips - 1

    dp = lax.axis_index("dp")
    y = dp // nx
    x = dp % nx

    def at_z(j):
        return {"seq": ((z + j + chips) % chips) * 2 + core}

    def across(j):
        return {"seq": ((z + j + chips) % chips) * 2 + 1 - core}

    def at_y(j):
        return {"dp": ((y + j) % ny) * nx + x}

    def at_x(j):
        return {"dp": y * nx + (x + j) % nx}

    barrier = pltpu.get_barrier_semaphore()
    peers = [across(j) for j in range(chips)]
    peers += [at_z(j) for j in range(1, chips)]
    peers += [at_y(j) for j in range(1, ny)]
    peers += [at_x(j) for j in range(1, nx)]
    for peer in peers:
        pl.semaphore_signal(barrier, inc=1, device_id=peer, device_id_type=MESH)

    def cols(h):
        return pl.ds(pl.multiple_of(h * size, size), size)

    def mate_copy(h):
        return remote(
            terms.at[role, h], mate.at[h], mate_send.at[h], mate_recv.at[h], {"seq": partner}
        )

    def chain_span(r):
        return pl.ds(r * (size // SPLIT), size // SPLIT)

    def chain_copy(h, r):
        n = h * SPLIT + r
        return remote(
            onward.at[h, chain_span(r)],
            chain.at[h, chain_span(r)],
            chain_send.at[n],
            chain_recv.at[n],
            {"seq": nxt},
        )

    def lent_copy(h):
        return remote(lend.at[h], lent.at[h], lent_send.at[h], lent_recv.at[h], {"seq": partner})

    def features(h):
        c = cols(h)
        fq = dot(q_ref[:, c], w_ref[0, h], 1, 0).astype(BF16)
        fk = dot(k_ref[:, c], w_ref[1, h], 1, 0).astype(BF16)
        fq_ref[:, c] = fq
        fk_ref[:, c] = fk
        terms[0, h] = dot(fk, v_ref[:, c], 0, 0)
        terms[1, h] = dot(fq, g_ref[:, c], 0, 0)

    features(0)
    features(1)
    pl.semaphore_wait(barrier, len(peers))

    @pl.when(first)
    def _():
        chain[...] = jnp.zeros_like(chain)

    mate_copy(0).start()
    mate_copy(1).start()

    def link(h):
        mate_copy(h).wait_recv()

        for r in range(SPLIT):
            span = chain_span(r)

            @pl.when(jnp.logical_not(first))
            def _():
                chain_copy(h, r).wait_recv()

            mine = chain[h, span]
            both = mine + terms[own, h, span]

            @pl.when(jnp.logical_not(last))
            def _():
                onward[h, span] = both + mate[h, span]
                chain_copy(h, r).start()

            lend[h, span] = both
            states[h, span] = mine.astype(BF16)

        lent_copy(h).start()

    lag = 3

    def start(i, carry):
        features(2 * i)
        features(2 * i + 1)
        mate_copy(2 * i).start()
        mate_copy(2 * i + 1).start()

        @pl.when(first & (i >= lag))
        def _():
            link(2 * (i - lag))
            link(2 * (i - lag) + 1)

        return carry

    lax.fori_loop(1, heads // 2, start, 0)

    causal = lax.broadcasted_iota(jnp.int32, (rows, rows), 0) >= lax.broadcasted_iota(
        jnp.int32, (rows, rows), 1
    )

    def masked(a, b):
        return jnp.where(causal, scale * dot(a, b, 1, 1), 0.0).astype(BF16)

    def block(h, side):
        return (h // nx) * (2 * nx) + side * nx + h % nx

    def pair_copy(d):
        return remote(
            wg_ref.at[pl.ds((1 - core) * chips, chips), d],
            pair.at[:, d],
            pair_send.at[d],
            pair_recv.at[d],
            {"seq": partner},
        )

    def query_side(h, state):
        c = cols(h)
        g = g_ref[:, c]
        qm = masked(g, v_ref[:, c])
        dfq = (scale * dot(g, state, 1, 1) + dot(qm, fk_ref[:, c], 1, 0)).astype(BF16)
        dq_ref[:, c] = dot(dfq, w_ref[0, h], 1, 1).astype(BF16)
        wg_ref[:, block(h, 0)] = dot(q_ref[:, c], dfq, 0, 0).reshape(rows // 8, 8, size)

    def key_side(h, state):
        c = cols(h)
        g = g_ref[:, c]
        v = v_ref[:, c]
        fq = fq_ref[:, c]
        fk = fk_ref[:, c]
        qm = masked(g, v)
        pm = masked(fq, fk)
        dfk = (scale * dot(v, state, 1, 1) + dot(qm, fq, 0, 0)).astype(BF16)
        dv_ref[:, c] = (scale * dot(fk, state, 1, 0) + dot(pm, g, 0, 0)).astype(BF16)
        dk_ref[:, c] = dot(dfk, w_ref[1, h], 1, 1).astype(BF16)
        wg_ref[:, block(h, 1)] = dot(k_ref[:, c], dfk, 0, 0).reshape(rows // 8, 8, size)

    def own_pair(i):
        @pl.when(role == 1)
        def _():
            for h in (2 * i, 2 * i + 1):
                query_side(h, states[h])

        @pl.when(role == 0)
        def _():
            for h in (2 * i, 2 * i + 1):
                key_side(h, states[h])

        for h in (2 * i, 2 * i + 1):
            pair_copy(block(h, 1 - role)).start()

    def lent_pair(i):
        lent_copy(2 * i).wait_recv()
        lent_copy(2 * i + 1).wait_recv()

        @pl.when(role == 0)
        def _():
            for h in (2 * i, 2 * i + 1):
                query_side(h, lent[h].astype(BF16))

        @pl.when(role == 1)
        def _():
            for h in (2 * i, 2 * i + 1):
                key_side(h, lent[h].astype(BF16))

        for h in (2 * i, 2 * i + 1):
            pair_copy(block(h, role)).start()

    early = jnp.clip(4 * hop - 2 * chips + 2, 0, heads // 2)

    def ahead(i, carry):
        @pl.when(i < early)
        def _():
            lent_pair(i)

        return carry

    lax.fori_loop(0, heads // 2, ahead, 0)

    def links(i, carry):
        @pl.when(jnp.logical_not(first) | (i >= heads // 2 - lag))
        def _():
            link(2 * i)
            link(2 * i + 1)

        @pl.when(last)
        def _():
            own_pair(i)

        return carry

    lax.fori_loop(0, heads // 2, links, 0)

    def gradients(i):
        @pl.when(jnp.logical_not(last))
        def _():
            own_pair(i)

        @pl.when(i >= early)
        def _():
            lent_pair(i)

    groups = heads // nx
    group = 2 * nx
    pairs = heads // 2 // groups
    ups = chips // 2
    downs = chips - 1 - ups

    def span_of(n):
        return pl.ds(pl.multiple_of(n * group, group), group)

    def local(j, span):
        t = (z + j) % chips
        return wg_ref[core * chips + t, span] + pair[t, span]

    def up_copy(step, n):
        span = span_of(n)
        return remote(
            up.at[step, span], up_in.at[step, span], up_send.at[step, n], up_recv.at[step, n], at_z(1)
        )

    def down_copy(step, n):
        span = span_of(n)
        return remote(
            down.at[step, span],
            down_in.at[step, span],
            down_send.at[step, n],
            down_recv.at[step, n],
            at_z(-1),
        )

    def advance(step, n):
        span = span_of(n)
        if step == 0:

            def arrived(d, carry):
                pair_copy(n * group + d).wait_recv()
                return carry

            lax.fori_loop(0, group, arrived, 0)
        if step < ups:
            value = local(ups - step, span)
            if step:
                up_copy(step - 1, n).wait_recv()
                value = value + up_in[step - 1, span]
            up[step, span] = value
            up_copy(step, n).start()
        if step < downs:
            value = local(chips - (downs - step), span)
            if step:
                down_copy(step - 1, n).wait_recv()
                value = value + down_in[step - 1, span]
            down[step, span] = value
            down_copy(step, n).start()
        if step == ups:
            up_copy(ups - 1, n).wait_recv()
            down_copy(downs - 1, n).wait_recv()
            mine_ref[span] = local(0, span) + up_in[ups - 1, span] + down_in[downs - 1, span]
            for side in range(2):
                there = side * groups + n

                @pl.when(there != y)
                def _():
                    y_copy((there - y + ny) % ny).start()

    def y_span(there):
        return pl.ds((there % groups) * group + (there // groups) * nx, nx)

    def y_copy(j):
        return remote(
            mine_ref.at[y_span((y + j) % ny)], y_in.at[j], y_send.at[j], y_recv.at[j], at_y(j)
        )

    def slot(s, carry):
        @pl.when(s < groups)
        def _():
            for p in range(pairs):
                gradients(pairs * s + p)

        for step in range(ups + 1):

            @pl.when((s >= step) & (s < step + groups))
            def _():
                advance(step, s - step)

        return carry

    lax.fori_loop(0, groups + ups, slot, 0)

    total = mine_ref[y_span(y)]
    for j in range(1, ny):
        y_copy(j).wait_recv()
        total = total + y_in[j]
    part[...] = total
    x_copies = []
    for j in range(1, nx):
        copy = remote(part.at[(x + j) % nx], x_in.at[j], x_send.at[j], x_recv.at[j], at_x(j))
        copy.start()
        x_copies.append(copy)
    total = part[x]
    for j in range(1, nx):
        x_copies[j - 1].wait_recv()
        total = total + x_in[j]
    whole[core, z] = total

    z_copies = []
    for j in range(chips // 2, -chips // 2, -1):
        for n, peer in enumerate((at_z, across)):
            if j or n:
                n = (j % chips) * 2 + n
                copy = remote(
                    whole.at[core, z], whole.at[core, z], z_send.at[n], z_recv.at[n], peer(j)
                )
                copy.start()
                z_copies.append(copy)

    def drain(h, carry):
        mate_copy(h).wait_send()
        lent_copy(h).wait_send()

        @pl.when(jnp.logical_not(last))
        def _():
            for r in range(SPLIT):
                chain_copy(h, r).wait_send()

        return carry

    lax.fori_loop(0, heads, drain, 0)

    def drain_blocks(d, carry):
        pair_copy(d).wait_send()
        return carry

    lax.fori_loop(0, 2 * heads, drain_blocks, 0)

    def drain_groups(n, carry):
        for step in range(ups):
            up_copy(step, n).wait_send()
        for step in range(downs):
            down_copy(step, n).wait_send()
        return carry

    lax.fori_loop(0, groups, drain_groups, 0)
    for j in range(1, ny):
        y_copy(j).wait_send()
    for copy in x_copies + z_copies:
        copy.wait_send()
    for copy in z_copies:
        copy.wait_recv()
    out_ref[...] = whole[...]


def attention(queries, keys_in, values_in, grad_out, feat_w, scale, chips, ny, nx):
    rows, width = queries.shape
    heads, size = feat_w.shape[1:3]
    vmem = pl.BlockSpec(memory_space=pltpu.VMEM)
    rowed = jax.ShapeDtypeStruct((rows, width), BF16)
    state = pltpu.VMEM((heads, size, size), F32)
    dma = pltpu.SemaphoreType.DMA
    ups = chips // 2
    downs = chips - 1 - ups
    blocks = 2 * heads
    sub = size // (2 * chips)

    def pieces(*lead):
        return pltpu.VMEM((*lead, sub, size), F32)

    return pl.pallas_call(
        functools.partial(attention_kernel, scale, chips, ny, nx),
        out_shape=[rowed] * 3 + [jax.ShapeDtypeStruct((2, chips, sub, size), F32)],
        in_specs=[vmem] * 5,
        out_specs=[vmem] * 4,
        scratch_shapes=[
            pltpu.VMEM((rows, width), BF16),
            pltpu.VMEM((rows, width), BF16),
            pltpu.VMEM((2, heads, size, size), F32),
            state,
            state,
            state,
            pltpu.VMEM((heads, size, size), BF16),
            state,
            state,
        ]
        + [dma((heads,))] * 2
        + [dma((heads * SPLIT,))] * 2
        + [dma((heads,))] * 2
        + [
            pieces(2 * chips, blocks),
            pieces(chips, blocks),
            pieces(ups, blocks),
            pieces(ups, blocks),
            pieces(downs, blocks),
            pieces(downs, blocks),
            pieces(blocks),
            pieces(ny, nx),
            pieces(nx),
            pieces(nx),
            pieces(2, chips),
        ]
        + [dma((blocks,))] * 2
        + [dma((ups, heads // nx))] * 2
        + [dma((downs, heads // nx))] * 2
        + [dma((ny,))] * 2
        + [dma((nx,))] * 2
        + [dma((2 * chips,))] * 2,
        compiler_params=pltpu.CompilerParams(collective_id=0, has_side_effects=True),
        name="attention",
    )(queries, keys_in, values_in, grad_out, feat_w)


def finish_kernel(gscale, a_ref, b_ref, c_ref, d_ref, oa_ref, ob_ref, oc_ref, od_ref):
    oa_ref[...] = a_ref[...]
    ob_ref[...] = b_ref[...]
    oc_ref[...] = c_ref[...]
    od_ref[...] = d_ref[...] * gscale


def finish(arrays, gscale, steps=2):
    specs = [
        pl.BlockSpec((a.shape[0] // steps, a.shape[1]), lambda i: (i, 0)) for a in arrays
    ]
    return pl.pallas_call(
        functools.partial(finish_kernel, gscale),
        grid=(steps,),
        out_shape=[jax.ShapeDtypeStruct(a.shape, a.dtype) for a in arrays],
        in_specs=specs,
        out_specs=specs,
        name="finish",
    )(*arrays)


def body(queries, keys_in, values_in, grad_out, feat_w):
    seq_count = lax.axis_size("seq")
    rep_count = lax.axis_size("dp")
    rows = queries.shape[1]
    hsize = feat_w.shape[2]
    scale = 1.0 / math.sqrt(hsize * rows * seq_count)
    gscale = 1.0 / math.sqrt(rows * seq_count * rep_count)
    nz = seq_count // 2
    nx = 4
    ny = rep_count // nx
    d_queries, d_keys, d_values, owned = attention(
        queries[0], keys_in[0], values_in[0], grad_out[0], feat_w, scale, nz, ny, nx
    )
    results = finish((d_queries, d_keys, d_values, owned.reshape(hsize, hsize)), gscale)
    return (results[0][None], results[1][None], results[2][None], results[3])


def solution(mesh):
    return jax.shard_map(
        body,
        mesh=mesh,
        in_specs=(
            P("dp", "seq", None),
            P("dp", "seq", None),
            P("dp", "seq", None),
            P("dp", "seq", None),
            P(),
        ),
        out_specs=(P("dp", "seq", None), P("dp", "seq", None), P("dp", "seq", None), P("dp", None)),
        check_vma=False,
    )
```
